256 devices in a mesh: mem: 32 (over z, x), space: 8 (over y, core).
Axes of the slice: x: 4, y: 4, z: 8, core: 2. Of those that a mesh axis runs over, the one named last changes fastest.
Arguments:
- params: float32 [256, 16, 16, 384], P('mem', 'space'), may hold values from -6 to 6
- start_field: float32 [16, 16, 384], P('space'), may hold values from -6 to 6
- obs_index: int32 [8192], P('space'), may hold values from 0 to 12287
- observed: float32 [8192], P('space'), may hold values from -16 to 16
- obs_noise: float32 [256, 8192], P('mem', 'space'), may hold values from -6 to 6
Outputs:
- updated: float32 [256, 16, 16, 384], P('mem', 'space')
- predicted: float32 [256, 8192], P('mem', 'space')
The draws below stay inside these ranges and needn't reach their ends.
Inputs may be any that keep to these rules, and one draw needn't show every extreme that they name: `obs_index`: each entry is the position, row by level by column, of a cell within the 2 rows of its own block; cells may repeat.
All inputs are finite; a program needn't handle non-finite values.
Results may differ from the reference program's by a relative error of at most 0.00025.
Values sent between devices are 32-bit elements; how exact they have to be, the bound alone decides.
A program may use at most 64 MiB of HBM per device.

```python
import jax
import jax.numpy as jnp
from jax import lax

ROWS_DEV = 2
LEV = 16
COLS = 384
OBS_DEV = 1024
NOBS = 8192
ROWS = 16
M = 256


def plant(entries, own_key, least, largest):
    shape = entries.shape
    spot = [jax.random.randint(jax.random.fold_in(own_key, axis), (), 0, shape[axis]) for axis in range(len(shape))]
    entries = entries.at[tuple(spot)].set(least)
    longest = shape.index(max(shape))
    spot[longest] = (spot[longest] + 1) % shape[longest]
    return entries.at[tuple(spot)].set(largest)


def levels(stream_key, shape, shards, smallest, high):
    factor_of, own = 1.0, jax.random.fold_in(stream_key, 6)
    for position, shards_of in shards:
        draws = jnp.exp(jax.random.uniform(jax.random.fold_in(own, position), (shards_of,), jnp.float32, smallest / len(shards), high / len(shards)))
        factor_of = factor_of * jnp.repeat(draws, shape[position] // shards_of).reshape([-1 if axis == position else 1 for axis in range(len(shape))])
    return factor_of


def bell_draw(own_key, dims, scale, most, shards=(), kind=jnp.bfloat16):
    values = scale * jax.random.normal(own_key, dims, jnp.float32)
    if shards:
        values = values * levels(own_key, dims, shards, -0.22, 0.18)
    return jnp.clip(values, -most, most).astype(kind)


def setup_inputs(seed: int = 0) -> dict:
    key_list = jax.random.split(jax.random.key(seed), 6)
    params = bell_draw(key_list[0], (M, ROWS, LEV, COLS), 1.0, 6.0, ((0, 32), (1, 8)), jnp.float32)
    start_field = bell_draw(key_list[1], (ROWS, LEV, COLS), 1.0, 6.0, ((0, 8),), jnp.float32)
    obs_index = plant(jax.random.randint(key_list[2], (NOBS,), 0, ROWS_DEV * LEV * COLS), jax.random.fold_in(key_list[2], 1), 0, (ROWS_DEV * LEV * COLS) - 1).astype(jnp.int32)
    observed = bell_draw(key_list[3], (NOBS,), 4.0, 16.0, ((0, 8),), jnp.float32)
    obs_noise = bell_draw(key_list[4], (M, NOBS), 1.0, 6.0, ((0, 32), (1, 8)), jnp.float32)
    return dict(params=params, start_field=start_field, obs_index=obs_index, observed=observed, obs_noise=obs_noise)


obs_variance = 0.02
step_weight = 0.25

def advance(field, diffusivity):
    padded = jnp.pad(field, ((1, 1), (0, 0), (1, 1)))
    laplace_sum = padded[2:, :, 1:-1] + padded[:-2, :, 1:-1] + padded[1:-1, :, 2:] + padded[1:-1, :, :-2] - 4.0 * field
    return field + step_weight * diffusivity * laplace_sum

def reference(params, start_field, obs_index, observed, obs_noise):
    highest = lax.Precision.HIGHEST
    plane = LEV * COLS
    shard_of = jnp.arange(NOBS, dtype=jnp.int32) // OBS_DEV
    global_row = shard_of * ROWS_DEV + obs_index // plane
    flat_index = (global_row * plane + obs_index % plane).astype(jnp.int32)

    def one_member(member_params):
        diffusivity = 0.1 + 0.8 * jax.nn.sigmoid(member_params)
        first_step = advance(start_field, diffusivity)
        second_step = advance(first_step, diffusivity)
        return second_step.reshape(-1)[flat_index]
    predicted = lax.map(one_member, params)
    spread = predicted - jnp.mean(predicted, axis=0)
    misfit = observed[None, :] + obs_noise - predicted
    gram_aa = jnp.dot(spread.astype(jnp.float32), spread.T.astype(jnp.float32), precision=highest, preferred_element_type=jnp.float32) / NOBS
    gram_ad = jnp.dot(spread.astype(jnp.float32), misfit.T.astype(jnp.float32), precision=highest, preferred_element_type=jnp.float32) / NOBS
    factor = jnp.linalg.cholesky(gram_aa + obs_variance * jnp.eye(M, dtype=jnp.float32))
    weights = jax.scipy.linalg.cho_solve((factor, True), gram_ad)
    param_avg = jnp.mean(params, axis=0)
    deviation = (params - param_avg).reshape(M, -1)
    shifted = jnp.dot(weights.T.astype(jnp.float32), deviation.astype(jnp.float32), precision=highest, preferred_element_type=jnp.float32)
    updated = params + shifted.reshape(params.shape)
    return (updated, predicted)
```

```python
import functools

import jax
import jax.numpy as jnp
from jax import lax
from jax.experimental import pallas as pl
from jax.experimental.pallas import tpu as pltpu
from jax.sharding import PartitionSpec as P

obs_variance = 0.02
step_weight = 0.25
x_size = 4
F32 = jnp.float32
BF16 = jnp.bfloat16


def product(left, right, dims):
    return lax.dot_general(
        left, right, (dims, ((), ())), precision=lax.Precision.HIGHEST, preferred_element_type=F32
    )


def mm(left, right):
    return product(left, right, ((1,), (0,)))


def shifted_cols(cells, amount):
    cols = cells.shape[-1]
    axis = cells.ndim - 1
    lane = lax.broadcasted_iota(jnp.int32, cells.shape, axis)
    if amount == 1:
        return jnp.where(lane == cols - 1, 0.0, pltpu.roll(cells, cols - 1, axis))
    return jnp.where(lane == 0, 0.0, pltpu.roll(cells, 1, axis))


def spd_inverse(matrix):
    n = matrix.shape[0]
    lane = lax.broadcasted_iota(jnp.int32, (1, n), 1)
    sub = lax.broadcasted_iota(jnp.int32, (n, 1), 0)

    def block(_, work):
        for t in range(8):
            row = work[t : t + 1, :]
            inv = 1.0 / row[:, t : t + 1]
            scaled = jnp.where(lane == t, inv, row * inv)
            col = work[:, t : t + 1]
            rest = jnp.where(lane == t, 0.0, work) - col * scaled
            work = jnp.where(sub == t, scaled, rest)
        work = pltpu.roll(work, n - 8, 1)
        return jnp.concatenate([work[8:], work[:8]], axis=0)

    return lax.fori_loop(0, n // 8, block, matrix)


def kernel(
    nm, ns, nobs_all,
    params_ref, start_ref, index_ref, observed_ref, noise_ref,
    updated_ref, predicted_ref,
    pt, dev, up_p, dn_p, up_s, dn_s, first_lap, second, noise_x, pred_x, pred_all,
    part, part_x, own_s, part_s, own_g, own_d, gz, gall, dz, dall, shift, back,
    send, recv,
):
    local, planes, cols = params_ref.shape
    levels = planes // 2
    members = nm * local
    nx = x_size
    nz = nm // nx
    obs = index_ref.shape[1]
    chunk = obs // nx
    cell_planes = planes // nm
    me_mem = lax.axis_index("mem")
    me_space = lax.axis_index("space")
    me_z = me_mem // nx
    me_x = me_mem % nx

    barrier = pltpu.get_barrier_semaphore()

    def hello_mem(d, c):
        pl.semaphore_signal(barrier, inc=1, device_id={"mem": (me_mem + d) % nm})
        return c

    def hello_space(d, c):
        pl.semaphore_signal(barrier, inc=1, device_id={"space": (me_space + d) % ns})
        return c

    lax.fori_loop(1, ns, hello_space, 0)
    lax.fori_loop(1, nm, hello_mem, 0)

    for b in range(planes // 8):
        block = params_ref[:, b * 8 : (b + 1) * 8, :]
        pt[b * 8 : (b + 1) * 8] = jnp.swapaxes(block, 0, 1)

    pl.semaphore_wait(barrier, (nm - 1) + (ns - 1))

    def put(src, dst, phase, device):
        pltpu.make_async_remote_copy(
            src_ref=src, dst_ref=dst, send_sem=send.at[phase], recv_sem=recv.at[phase],
            device_id=device,
        ).start()

    def arrived(ref, phase):
        pltpu.make_async_copy(ref, ref, recv.at[phase]).wait()

    def sent(ref, phase):
        pltpu.make_async_copy(ref, ref, send.at[phase]).wait()

    below = {"space": (me_space + 1) % ns}
    above = {"space": (me_space + ns - 1) % ns}
    put(start_ref, up_s, 0, below)
    put(start_ref, dn_s, 1, above)
    put(pt.at[pl.ds(levels, levels)], up_p, 2, below)
    put(pt.at[pl.ds(0, levels)], dn_p, 3, above)

    def x_peer(d):
        peer = (me_x + d) % nx
        return peer, {"mem": me_z * nx + peer}

    def z_peer(d):
        peer = (me_z + d) % nz
        return peer, {"mem": peer * nx + me_x}

    def to_chunk(ref, peer):
        return ref.at[:, pl.ds(pl.multiple_of(peer * chunk, chunk), chunk)]

    for d in range(1, nx):
        peer, device = x_peer(d)
        put(to_chunk(noise_ref, peer), noise_x.at[me_x], 4, device)
    noise_x[me_x] = noise_ref[:, pl.ds(pl.multiple_of(me_x * chunk, chunk), chunk)]

    def send_params(d, c):
        peer = (me_mem + d) % nm
        put(
            pt.at[pl.ds(peer * cell_planes, cell_planes)],
            dev.at[me_mem],
            5,
            {"mem": peer},
        )
        return c

    lax.fori_loop(1, nm, send_params, 0)
    dev[me_mem] = pt[pl.ds(me_mem * cell_planes, cell_planes)]

    def diffusivity(cells):
        return 0.1 + 0.8 / (1.0 + jnp.exp(-cells))

    arrived(up_s, 0)
    arrived(dn_s, 1)
    has_up = me_space > 0
    has_down = me_space < ns - 1
    zero = jnp.zeros((levels, cols), F32)
    state = [
        jnp.where(has_up, up_s[0], zero),
        jnp.where(has_up, up_s[1], zero),
        start_ref[0],
        start_ref[1],
        jnp.where(has_down, dn_s[0], zero),
        jnp.where(has_down, dn_s[1], zero),
    ]
    for r in range(4):
        mid = state[r + 1]
        first_lap[0, r] = mid
        first_lap[1, r] = step_weight * (
            state[r + 2] + state[r] + shifted_cols(mid, 1) + shifted_cols(mid, -1) - 4.0 * mid
        )
    arrived(up_p, 2)
    arrived(dn_p, 3)

    for level in range(levels):
        cells = [up_p[level], pt[level], pt[levels + level], dn_p[level]]
        diffs = [diffusivity(c) for c in cells]
        firsts = [
            first_lap[0, r, level : level + 1, :] + diffs[r] * first_lap[1, r, level : level + 1, :]
            for r in range(4)
        ]
        firsts[0] = jnp.where(has_up, firsts[0], 0.0)
        firsts[3] = jnp.where(has_down, firsts[3], 0.0)
        for r in range(2):
            mid = firsts[r + 1]
            lap = firsts[r + 2] + firsts[r] + shifted_cols(mid, 1) + shifted_cols(mid, -1) - 4.0 * mid
            second[r * levels + level] = mid + step_weight * diffs[r + 1] * lap

    blocks = cols // 128
    pieces = []
    for b in range(blocks):
        block = second[:, :, b * 128 : (b + 1) * 128].reshape(planes * local, 128)
        high = block.astype(BF16)
        left = block - high.astype(F32)
        mid = left.astype(BF16)
        low = (left - mid.astype(F32)).astype(BF16)
        pieces.append(jnp.concatenate([high, mid, low], axis=1))
    for c in range(nx):
        where = index_ref[:, c * chunk : (c + 1) * chunk]
        lane_of = where % 128
        block_of = where // 128
        hot = (lax.broadcasted_iota(jnp.int32, (128, chunk), 0) == lane_of).astype(F32).astype(BF16)
        hot = jnp.concatenate([hot, hot, hot], axis=0)
        total = jnp.zeros((local, chunk), F32)
        for b in range(blocks):
            picked = jnp.dot(pieces[b], hot, preferred_element_type=F32)
            for p in range(planes):
                total = total + jnp.where(
                    block_of == p * blocks + b, picked[p * local : (p + 1) * local], 0.0
                )
        predicted_ref[:, c * chunk : (c + 1) * chunk] = total

    for d in range(1, nx):
        peer, device = x_peer(d)
        put(to_chunk(predicted_ref, peer), pred_x.at[me_x], 6, device)
    pred_x[me_x] = predicted_ref[:, pl.ds(pl.multiple_of(me_x * chunk, chunk), chunk)]
    arrived(pred_x.at[pl.ds(0, nx - 1)], 6)

    for d in range(1, nz):
        peer, device = z_peer(d)
        put(pred_x, pred_all.at[me_z], 7, device)
    pred_own = pred_x[...].reshape(nx * local, chunk)
    pred_all[me_z] = pred_x[...]
    arrived(noise_x.at[pl.ds(0, nx - 1)], 4)
    seen = observed_ref[:, pl.ds(pl.multiple_of(me_x * chunk, chunk), chunk)]
    misfit = seen + noise_x[...].reshape(nx * local, chunk) - pred_own
    arrived(pred_all.at[pl.ds(0, nz - 1)], 7)

    everyone = pred_all[...].reshape(members, chunk)
    mean = jnp.sum(everyone, axis=0, keepdims=True) * (1.0 / members)
    spread = everyone - mean
    spread_own = pred_own - mean
    rows = []
    for x in range(nx):
        rows += [spread_own[x * local : (x + 1) * local], misfit[x * local : (x + 1) * local]]
    gram = product(jnp.concatenate(rows, axis=0), spread, ((1,), (1,)))
    part[...] = gram.reshape(nx, 2 * local, members)

    for d in range(1, nx):
        peer, device = x_peer(d)
        put(part.at[peer], part_x.at[me_x], 8, device)
    part_x[me_x] = part[me_x]
    arrived(part_x.at[pl.ds(0, nx - 1)], 8)
    own_s[...] = jnp.sum(part_x[...], axis=0)

    for d in range(1, ns):
        put(own_s, part_s.at[me_space], 9, {"space": (me_space + d) % ns})
    part_s[me_space] = own_s[...]
    arrived(part_s.at[pl.ds(0, ns - 1)], 9)
    total = jnp.sum(part_s[...], axis=0) * (1.0 / nobs_all)
    own_g[...] = total[:local]
    own_d[...] = total[local:]

    for d in range(1, nz):
        peer, device = z_peer(d)
        put(own_g, gz.at[me_z], 10, device)
    for d in range(1, nz):
        peer, device = z_peer(d)
        put(own_d, dz.at[me_z], 11, device)
    gz[me_z] = own_g[...]
    dz[me_z] = own_d[...]
    arrived(gz.at[pl.ds(0, nz - 1)], 10)
    for d in range(1, nx):
        peer, device = x_peer(d)
        put(gz, gall.at[:, me_x], 12, device)
    gall[:, me_x] = gz[...]
    arrived(dz.at[pl.ds(0, nz - 1)], 11)
    for d in range(1, nx):
        peer, device = x_peer(d)
        put(dz, dall.at[:, me_x], 13, device)
    dall[:, me_x] = dz[...]

    arrived(dev.at[pl.ds(0, nm - 1)], 5)
    width = cell_planes * cols
    deviation = jnp.concatenate(
        [dev[:, p].reshape(members, cols) for p in range(cell_planes)], axis=1
    )
    deviation = deviation - jnp.sum(deviation, axis=0, keepdims=True) * (1.0 / members)

    arrived(gall.at[:, pl.ds(0, nx - 1)], 12)
    half = members // 2
    system = gall[...].reshape(members, members)
    eye = lax.broadcasted_iota(jnp.int32, (members, members), 0) == lax.broadcasted_iota(
        jnp.int32, (members, members), 1
    )
    system = system + jnp.where(eye, obs_variance, 0.0)
    upper = system[:half, half:]
    inv_a = spd_inverse(system[:half, :half])
    lower = mm(system[half:, :half], inv_a)
    inv_b = spd_inverse(system[half:, half:] - mm(lower, upper))
    dev_a, dev_b = deviation[:half], deviation[half:]
    sol_b = mm(inv_b, dev_b - mm(lower, dev_a))
    sol_a = mm(inv_a, dev_a) - product(lower, sol_b, ((0,), (0,)))
    arrived(dall.at[:, pl.ds(0, nx - 1)], 13)
    gains = dall[...].reshape(members, members)
    moved = mm(gains[:, :half], sol_a) + mm(gains[:, half:], sol_b)
    for p in range(cell_planes):
        shift[:, p] = moved[:, p * cols : (p + 1) * cols].reshape(nm, local, cols)

    def send_back(d, c):
        peer = (me_mem + d) % nm
        put(
            shift.at[peer],
            back.at[pl.ds(me_mem * cell_planes, cell_planes)],
            14,
            {"mem": peer},
        )
        return c

    lax.fori_loop(1, nm, send_back, 0)
    back[pl.ds(me_mem * cell_planes, cell_planes)] = shift[me_mem]

    sent(start_ref, 0)
    sent(start_ref, 1)
    sent(up_p, 2)
    sent(dn_p, 3)
    sent(noise_x.at[pl.ds(0, nx - 1)], 4)
    sent(dev.at[pl.ds(0, nm - 1)], 5)
    sent(pred_x.at[pl.ds(0, nx - 1)], 6)
    sent(pred_all.at[pl.ds(0, nz - 1)], 7)
    sent(part_x.at[pl.ds(0, nx - 1)], 8)
    sent(part_s.at[pl.ds(0, ns - 1)], 9)
    sent(gz.at[pl.ds(0, nz - 1)], 10)
    sent(dz.at[pl.ds(0, nz - 1)], 11)
    sent(gall.at[:, pl.ds(0, nx - 1)], 12)
    sent(dall.at[:, pl.ds(0, nx - 1)], 13)
    sent(back.at[pl.ds(0, (nm - 1) * cell_planes)], 14)

    arrived(back.at[pl.ds(0, (nm - 1) * cell_planes)], 14)
    for b in range(planes // 8):
        block = jnp.swapaxes(back[b * 8 : (b + 1) * 8], 0, 1)
        updated_ref[:, b * 8 : (b + 1) * 8, :] = params_ref[:, b * 8 : (b + 1) * 8, :] + block


def per_device(params, start_field, obs_index, observed, obs_noise):
    local, rows, levels, cols = params.shape
    nm, ns = lax.axis_size("mem"), lax.axis_size("space")
    obs = obs_index.shape[0]
    members = nm * local
    nx = x_size
    nz = nm // nx
    chunk = obs // nx
    planes = rows * levels
    cell_planes = planes // nm
    vmem = pl.BlockSpec(memory_space=pltpu.VMEM)
    shapes = [
        (planes, local, cols),
        (nm, cell_planes, local, cols),
        (levels, local, cols),
        (levels, local, cols),
        (rows, levels, cols),
        (rows, levels, cols),
        (2, 4, levels, cols),
        (planes, local, cols),
        (nx, local, chunk),
        (nx, local, chunk),
        (nz, nx, local, chunk),
        (nx, 2 * local, members),
        (nx, 2 * local, members),
        (2 * local, members),
        (ns, 2 * local, members),
        (local, members),
        (local, members),
        (nz, local, members),
        (nz, nx, local, members),
        (nz, local, members),
        (nz, nx, local, members),
        (nm, cell_planes, local, cols),
        (planes, local, cols),
    ]
    updated, predicted = pl.pallas_call(
        functools.partial(kernel, nm, ns, obs * ns),
        out_shape=(
            jax.ShapeDtypeStruct((local, planes, cols), F32),
            jax.ShapeDtypeStruct((local, obs), F32),
        ),
        in_specs=[vmem] * 5,
        out_specs=(vmem, vmem),
        scratch_shapes=[pltpu.VMEM(s, F32) for s in shapes]
        + [pltpu.SemaphoreType.DMA((15,)), pltpu.SemaphoreType.DMA((15,))],
        compiler_params=pltpu.CompilerParams(collective_id=0, has_side_effects=True),
    )(
        params.reshape(local, planes, cols),
        start_field,
        obs_index.reshape(1, obs),
        observed.reshape(1, obs),
        obs_noise,
    )
    return updated.reshape(params.shape), predicted


def solution(mesh):
    in_specs = (
        P("mem", "space", None, None),
        P("space", None, None),
        P("space"),
        P("space"),
        P("mem", "space"),
    )
    out_specs = (P("mem", "space", None, None), P("mem", "space"))
    return jax.shard_map(
        per_device, mesh=mesh, in_specs=in_specs, out_specs=out_specs, check_vma=False
    )
```

```python
import functools

import jax
import jax.numpy as jnp
from jax import lax
from jax.experimental import pallas as pl
from jax.experimental.pallas import tpu as pltpu
from jax.sharding import PartitionSpec as P

obs_variance = 0.02
step_weight = 0.25
x_size = 4
F32 = jnp.float32
BF16 = jnp.bfloat16


def product(left, right, dims):
    return lax.dot_general(
        left, right, (dims, ((), ())), precision=lax.Precision.HIGHEST, preferred_element_type=F32
    )


def mm(left, right):
    return product(left, right, ((1,), (0,)))


def shifted_cols(cells, amount):
    cols = cells.shape[-1]
    axis = cells.ndim - 1
    lane = lax.broadcasted_iota(jnp.int32, cells.shape, axis)
    if amount == 1:
        return jnp.where(lane == cols - 1, 0.0, pltpu.roll(cells, cols - 1, axis))
    return jnp.where(lane == 0, 0.0, pltpu.roll(cells, 1, axis))


def swept_rows(rows):
    count, n = rows.shape
    sub = lax.broadcasted_iota(jnp.int32, rows.shape, 0)
    lane = lax.broadcasted_iota(jnp.int32, rows.shape, 1)
    entry = {}
    for j in range(count):
        col = jnp.broadcast_to(rows[:, j : j + 1], rows.shape)
        for i in range(j, count):
            entry[i, j] = jnp.broadcast_to(col[i : i + 1], rows.shape)

    def at(i, j):
        return entry[max(i, j), min(i, j)]

    for k in range(count):
        inv = 1.0 / entry[k, k]
        others = [i for i in range(count) if i != k]
        old = {i: at(i, k) for i in others}
        new = {i: old[i] * inv for i in others}
        for j in others:
            for i in others:
                if i >= j:
                    entry[i, j] = entry[i, j] - new[i] * old[j]
        for i in others:
            entry[max(i, k), min(i, k)] = new[i]
        entry[k, k] = -inv

    total = jnp.zeros(rows.shape, F32)
    corner = total
    for j in range(count):
        col = at(0, j)
        for i in range(1, count):
            col = jnp.where(sub == i, at(i, j), col)
        total = total - col * rows[j : j + 1]
        corner = jnp.where(lane == j, col, corner)
    return jnp.where(lane < count, corner, total)


def spd_inverse(matrix):
    n = matrix.shape[0]
    lane = lax.broadcasted_iota(jnp.int32, (1, n), 1)

    def block(_, work):
        head = swept_rows(work[:8])
        rest = work[8:]
        tail = jnp.where(lane < 8, 0.0, rest)
        for t in range(8):
            tail = tail - rest[:, t : t + 1] * head[t : t + 1]
        return jnp.concatenate([pltpu.roll(tail, n - 8, 1), pltpu.roll(head, n - 8, 1)], axis=0)

    return -lax.fori_loop(0, n // 8, block, matrix)


def kernel(
    nm, ns, nobs_all,
    params_ref, start_ref, index_ref, observed_ref, noise_ref,
    shift_ref, predicted_ref,
    pt, dev, up_p, dn_p, up_s, dn_s, first_lap, second, noise_x, pred_all,
    part_g, part_m, part_gx, part_mx, own_g, own_m, part_gs, part_ms, rows_a, rows_b, rows_m,
    gram_a, gram_b, gains_all, shift, back,
    send, recv, rounds,
):
    local, planes, cols = params_ref.shape
    levels = planes // 2
    members = nm * local
    half = members // 2
    nx = x_size
    nz = nm // nx
    obs = index_ref.shape[1]
    chunk = obs // nx
    cell_planes = planes // nm
    me_mem = lax.axis_index("mem")
    me_space = lax.axis_index("space")
    me_z = me_mem // nx
    me_x = me_mem % nx

    def space_peer(d):
        return {"space": (me_space + d) % ns}

    def x_peer(d):
        peer = (me_x + d) % nx
        return peer, {"mem": me_z * nx + peer}

    def z_peer(d):
        return {"mem": (me_z + d) % nz * nx + me_x}

    barrier = pltpu.get_barrier_semaphore()
    nearby = [space_peer(1), space_peer(ns - 1), z_peer(1), z_peer(nz - 1)]
    greeted = nearby + [x_peer(d)[1] for d in range(1, nx)]
    for device in greeted:
        pl.semaphore_signal(barrier, inc=1, device_id=device)

    for b in range(planes // 8):
        pt[b * 8 : (b + 1) * 8] = jnp.swapaxes(params_ref[:, b * 8 : (b + 1) * 8, :], 0, 1)

    pl.semaphore_wait(barrier, len(greeted))

    def put(src, dst, phase, device):
        pltpu.make_async_remote_copy(
            src_ref=src, dst_ref=dst, send_sem=send.at[phase], recv_sem=recv.at[phase],
            device_id=device,
        ).start()

    def arrived(ref, phase):
        pltpu.make_async_copy(ref, ref, recv.at[phase]).wait()

    def sent(ref, phase):
        pltpu.make_async_copy(ref, ref, send.at[phase]).wait()

    def put_all(pick, dst, phase):
        def body(t, c):
            q = t // nx
            dz = nz // 2 + (1 - 2 * (q % 2)) * ((q + 1) // 2)
            peer = (me_z + dz) % nz * nx + (me_x + t + 1) % nx
            put(pick(peer), dst, phase, {"mem": peer})
            return c

        lax.fori_loop(0, nm - 1, body, 0)

    def greet(devices, step):
        for device in devices:
            pl.semaphore_signal(rounds.at[step], inc=1, device_id=device)

    put(start_ref, up_s, 0, space_peer(1))
    put(start_ref, dn_s, 1, space_peer(ns - 1))
    put(pt.at[pl.ds(levels, levels)], up_p, 2, space_peer(1))
    put(pt.at[pl.ds(0, levels)], dn_p, 3, space_peer(ns - 1))
    greet(nearby, 0)

    def to_chunk(ref, peer):
        return ref.at[:, pl.ds(pl.multiple_of(peer * chunk, chunk), chunk)]

    for d in range(1, nx):
        peer, device = x_peer(d)
        put(to_chunk(noise_ref, peer), noise_x.at[me_x], 4, device)
    noise_x[me_x] = noise_ref[:, pl.ds(pl.multiple_of(me_x * chunk, chunk), chunk)]
    dev[me_mem] = pt[pl.ds(me_mem * cell_planes, cell_planes)]

    pl.semaphore_wait(rounds.at[0], 4)
    greet([space_peer(2), space_peer(ns - 2), z_peer(2), z_peer(nz - 2)], 1)

    def diffusivity(cells):
        return 0.1 + 0.8 / (1.0 + jnp.exp(-cells))

    arrived(up_s, 0)
    arrived(dn_s, 1)
    has_up = me_space > 0
    has_down = me_space < ns - 1
    zero = jnp.zeros((levels, cols), F32)
    state = [
        jnp.where(has_up, up_s[0], zero),
        jnp.where(has_up, up_s[1], zero),
        start_ref[0],
        start_ref[1],
        jnp.where(has_down, dn_s[0], zero),
        jnp.where(has_down, dn_s[1], zero),
    ]
    for r in range(4):
        mid = state[r + 1]
        first_lap[0, r] = mid
        first_lap[1, r] = step_weight * (
            state[r + 2] + state[r] + shifted_cols(mid, 1) + shifted_cols(mid, -1) - 4.0 * mid
        )
    pl.semaphore_wait(rounds.at[1], 4)
    greet([z_peer(nz // 2)], 2)
    arrived(up_p, 2)
    arrived(dn_p, 3)

    for level in range(levels):
        cells = [up_p[level], pt[level], pt[levels + level], dn_p[level]]
        diffs = [diffusivity(c) for c in cells]
        firsts = [
            first_lap[0, r, level : level + 1, :] + diffs[r] * first_lap[1, r, level : level + 1, :]
            for r in range(4)
        ]
        firsts[0] = jnp.where(has_up, firsts[0], 0.0)
        firsts[3] = jnp.where(has_down, firsts[3], 0.0)
        for r in range(2):
            mid = firsts[r + 1]
            lap = firsts[r + 2] + firsts[r] + shifted_cols(mid, 1) + shifted_cols(mid, -1) - 4.0 * mid
            second[r * levels + level] = mid + step_weight * diffs[r + 1] * lap

    blocks = cols // 128
    pieces = []
    for b in range(blocks):
        block = second[:, :, b * 128 : (b + 1) * 128].reshape(planes * local, 128)
        high = block.astype(BF16)
        left = block - high.astype(F32)
        mid = left.astype(BF16)
        low = (left - mid.astype(F32)).astype(BF16)
        pieces.append(jnp.concatenate([high, mid, low], axis=1))
    for c in range(nx):
        where = index_ref[:, c * chunk : (c + 1) * chunk]
        lane_of = where % 128
        block_of = where // 128
        hot = (lax.broadcasted_iota(jnp.int32, (128, chunk), 0) == lane_of).astype(F32).astype(BF16)
        hot = jnp.concatenate([hot, hot, hot], axis=0)
        total = jnp.zeros((local, chunk), F32)
        for b in range(blocks):
            picked = jnp.dot(pieces[b], hot, preferred_element_type=F32)
            for p in range(planes):
                total = total + jnp.where(
                    block_of == p * blocks + b, picked[p * local : (p + 1) * local], 0.0
                )
        predicted_ref[:, c * chunk : (c + 1) * chunk] = total

    pl.semaphore_wait(rounds.at[2], 1)
    put_all(lambda peer: to_chunk(predicted_ref, peer % nx), pred_all.at[me_mem], 5)
    pred_all[me_mem] = predicted_ref[:, pl.ds(pl.multiple_of(me_x * chunk, chunk), chunk)]
    arrived(noise_x.at[pl.ds(0, nx - 1)], 4)
    seen = observed_ref[:, pl.ds(pl.multiple_of(me_x * chunk, chunk), chunk)]
    target = seen + noise_x[...].reshape(nx * local, chunk)
    arrived(pred_all.at[pl.ds(0, nm - 1)], 5)

    everyone = pred_all[...].reshape(members, chunk)
    pred_own = pred_all[pl.ds(me_z * nx, nx)].reshape(nx * local, chunk)
    mean = jnp.sum(everyone, axis=0, keepdims=True) * (1.0 / members)
    spread = everyone - mean
    part_g[...] = product(pred_own - mean, spread, ((1,), (1,))).reshape(nx, local, members)
    for d in range(1, nx):
        peer, device = x_peer(d)
        put(part_g.at[peer], part_gx.at[me_x], 6, device)
    part_m[...] = product(target - pred_own, spread, ((1,), (1,))).reshape(nx, local, members)
    for d in range(1, nx):
        peer, device = x_peer(d)
        put(part_m.at[peer], part_mx.at[me_x], 7, device)
    part_gx[me_x] = part_g[me_x]
    part_mx[me_x] = part_m[me_x]

    arrived(part_gx.at[pl.ds(0, nx - 1)], 6)
    own_g[...] = jnp.sum(part_gx[...], axis=0)
    for d in range(1, ns):
        put(own_g, part_gs.at[me_space], 8, space_peer(d))
    part_gs[me_space] = own_g[...]
    arrived(part_mx.at[pl.ds(0, nx - 1)], 7)
    own_m[...] = jnp.sum(part_mx[...], axis=0)
    for d in range(1, ns):
        put(own_m, part_ms.at[me_space], 9, space_peer(d))
    part_ms[me_space] = own_m[...]

    arrived(part_gs.at[pl.ds(0, ns - 1)], 8)
    total = jnp.sum(part_gs[...], axis=0) * (1.0 / nobs_all)
    rows_a[...] = total[:, :half]
    rows_b[...] = total[:, half:]
    leading = me_z < nz // 2

    @pl.when(leading)
    def _():
        put_all(lambda peer: rows_a, gram_a.at[me_mem], 10)
        gram_a[me_mem] = rows_a[...]

    put_all(lambda peer: rows_b, gram_b.at[me_mem], 11)
    gram_b[me_mem] = rows_b[...]

    arrived(part_ms.at[pl.ds(0, ns - 1)], 9)
    rows_m[...] = jnp.sum(part_ms[...], axis=0) * (1.0 / nobs_all)
    put_all(lambda peer: rows_m, gains_all.at[me_mem], 12)
    gains_all[me_mem] = rows_m[...]
    put_all(lambda peer: pt.at[pl.ds(peer * cell_planes, cell_planes)], dev.at[me_mem], 13)

    @pl.when(leading)
    def _():
        arrived(gram_a.at[pl.ds(0, nm // 2 - 1)], 10)

    @pl.when(jnp.logical_not(leading))
    def _():
        arrived(gram_a, 10)

    eye = lax.broadcasted_iota(jnp.int32, (half, half), 0) == lax.broadcasted_iota(
        jnp.int32, (half, half), 1
    )
    ridge = jnp.where(eye, obs_variance, 0.0)
    inv_a = spd_inverse(gram_a[...].reshape(half, half) + ridge)
    arrived(gram_b.at[pl.ds(0, nm - 1)], 11)
    right = gram_b[...].reshape(members, half)
    upper = right[:half]
    lower = product(upper, inv_a, ((0,), (0,)))
    inv_b = spd_inverse(right[half:] + ridge - mm(lower, upper))

    arrived(dev.at[pl.ds(0, nm - 1)], 13)
    deviation = jnp.concatenate(
        [dev[:, p].reshape(members, cols) for p in range(cell_planes)], axis=1
    )
    deviation = deviation - jnp.sum(deviation, axis=0, keepdims=True) * (1.0 / members)
    dev_a, dev_b = deviation[:half], deviation[half:]
    sol_b = mm(inv_b, dev_b - mm(lower, dev_a))
    sol_a = mm(inv_a, dev_a) - product(lower, sol_b, ((0,), (0,)))
    arrived(gains_all.at[pl.ds(0, nm - 1)], 12)
    gains = gains_all[...].reshape(members, members)
    moved = mm(gains[:, :half], sol_a) + mm(gains[:, half:], sol_b)
    for p in range(cell_planes):
        shift[:, p] = moved[:, p * cols : (p + 1) * cols].reshape(nm, local, cols)

    put_all(lambda peer: shift.at[peer], back.at[pl.ds(me_mem * cell_planes, cell_planes)], 14)
    back[pl.ds(me_mem * cell_planes, cell_planes)] = shift[me_mem]

    sent(start_ref, 0)
    sent(start_ref, 1)
    sent(up_p, 2)
    sent(dn_p, 3)
    sent(noise_x.at[pl.ds(0, nx - 1)], 4)
    sent(pred_all.at[pl.ds(0, nm - 1)], 5)
    sent(part_gx.at[pl.ds(0, nx - 1)], 6)
    sent(part_mx.at[pl.ds(0, nx - 1)], 7)
    sent(part_gs.at[pl.ds(0, ns - 1)], 8)
    sent(part_ms.at[pl.ds(0, ns - 1)], 9)

    @pl.when(leading)
    def _():
        sent(gram_b.at[pl.ds(0, nm - 1)], 10)

    sent(gram_b.at[pl.ds(0, nm - 1)], 11)
    sent(gains_all.at[pl.ds(0, nm - 1)], 12)
    sent(dev.at[pl.ds(0, nm - 1)], 13)
    sent(back.at[pl.ds(0, (nm - 1) * cell_planes)], 14)

    arrived(back.at[pl.ds(0, (nm - 1) * cell_planes)], 14)
    for b in range(planes // 8):
        shift_ref[:, b * 8 : (b + 1) * 8, :] = jnp.swapaxes(back[b * 8 : (b + 1) * 8], 0, 1)


def per_device(params, start_field, obs_index, observed, obs_noise):
    local, rows, levels, cols = params.shape
    nm, ns = lax.axis_size("mem"), lax.axis_size("space")
    obs = obs_index.shape[0]
    members = nm * local
    nx = x_size
    chunk = obs // nx
    planes = rows * levels
    cell_planes = planes // nm
    vmem = pl.BlockSpec(memory_space=pltpu.VMEM)
    half = members // 2
    shapes = [
        (planes, local, cols),
        (nm, cell_planes, local, cols),
        (levels, local, cols),
        (levels, local, cols),
        (rows, levels, cols),
        (rows, levels, cols),
        (2, 4, levels, cols),
        (planes, local, cols),
        (nx, local, chunk),
        (nm, local, chunk),
        (nx, local, members),
        (nx, local, members),
        (nx, local, members),
        (nx, local, members),
        (local, members),
        (local, members),
        (ns, local, members),
        (ns, local, members),
        (local, half),
        (local, half),
        (local, members),
        (nm // 2, local, half),
        (nm, local, half),
        (nm, local, members),
        (nm, cell_planes, local, cols),
        (planes, local, cols),
    ]
    shift, predicted = pl.pallas_call(
        functools.partial(kernel, nm, ns, obs * ns),
        out_shape=(
            jax.ShapeDtypeStruct((local, planes, cols), F32),
            jax.ShapeDtypeStruct((local, obs), F32),
        ),
        in_specs=[vmem] * 5,
        out_specs=(vmem, vmem),
        scratch_shapes=[pltpu.VMEM(s, F32) for s in shapes]
        + [pltpu.SemaphoreType.DMA((15,)), pltpu.SemaphoreType.DMA((15,)), pltpu.SemaphoreType.REGULAR((3,))],
        compiler_params=pltpu.CompilerParams(collective_id=0, has_side_effects=True),
    )(
        params.reshape(local, planes, cols),
        start_field,
        obs_index.reshape(1, obs),
        observed.reshape(1, obs),
        obs_noise,
    )
    return params + shift.reshape(params.shape), predicted


def solution(mesh):
    in_specs = (
        P("mem", "space", None, None),
        P("space", None, None),
        P("space"),
        P("space"),
        P("mem", "space"),
    )
    out_specs = (P("mem", "space", None, None), P("mem", "space"))
    return jax.shard_map(
        per_device, mesh=mesh, in_specs=in_specs, out_specs=out_specs, check_vma=False
    )
```

```python
import functools

import jax
import jax.numpy as jnp
from jax import lax
from jax.experimental import pallas as pl
from jax.experimental.pallas import tpu as pltpu
from jax.sharding import PartitionSpec as P

obs_variance = 0.02
step_weight = 0.25
x_size = 4
F32 = jnp.float32
BF16 = jnp.bfloat16


def product(left, right, dims):
    return lax.dot_general(
        left, right, (dims, ((), ())), precision=lax.Precision.HIGHEST, preferred_element_type=F32
    )


def mm(left, right):
    return product(left, right, ((1,), (0,)))


def shifted_cols(cells, amount):
    cols = cells.shape[-1]
    axis = cells.ndim - 1
    lane = lax.broadcasted_iota(jnp.int32, cells.shape, axis)
    if amount == 1:
        return jnp.where(lane == cols - 1, 0.0, pltpu.roll(cells, cols - 1, axis))
    return jnp.where(lane == 0, 0.0, pltpu.roll(cells, 1, axis))


def swept_rows(rows):
    count, n = rows.shape
    sub = lax.broadcasted_iota(jnp.int32, rows.shape, 0)
    lane = lax.broadcasted_iota(jnp.int32, rows.shape, 1)
    entry = {}
    for j in range(count):
        col = jnp.broadcast_to(rows[:, j : j + 1], rows.shape)
        for i in range(j, count):
            entry[i, j] = jnp.broadcast_to(col[i : i + 1], rows.shape)

    def at(i, j):
        return entry[max(i, j), min(i, j)]

    for k in range(count):
        inv = 1.0 / entry[k, k]
        others = [i for i in range(count) if i != k]
        old = {i: at(i, k) for i in others}
        new = {i: old[i] * inv for i in others}
        for j in others:
            for i in others:
                if i >= j:
                    entry[i, j] = entry[i, j] - new[i] * old[j]
        for i in others:
            entry[max(i, k), min(i, k)] = new[i]
        entry[k, k] = -inv

    total = jnp.zeros(rows.shape, F32)
    corner = total
    for j in range(count):
        col = at(0, j)
        for i in range(1, count):
            col = jnp.where(sub == i, at(i, j), col)
        total = total - col * rows[j : j + 1]
        corner = jnp.where(lane == j, col, corner)
    return jnp.where(lane < count, corner, total)


def spd_inverse(matrix):
    n = matrix.shape[0]
    lane = lax.broadcasted_iota(jnp.int32, (1, n), 1)

    def block(_, work):
        head = swept_rows(work[:8])
        rest = work[8:]
        tail = jnp.where(lane < 8, 0.0, rest)
        for t in range(8):
            tail = tail - rest[:, t : t + 1] * head[t : t + 1]
        return jnp.concatenate([pltpu.roll(tail, n - 8, 1), pltpu.roll(head, n - 8, 1)], axis=0)

    return -lax.fori_loop(0, n // 8, block, matrix)


def kernel(
    nm, ns, nobs_all,
    params_ref, start_ref, index_ref, observed_ref, noise_ref,
    shift_ref, predicted_ref,
    pt, dev, up_p, dn_p, up_s, dn_s, first_lap, second, noise_x, pred_all,
    part_g, part_m, part_gx, part_mx, own_g, own_m, part_gs, part_ms, rows_a, rows_b, rows_m,
    gram_a, gram_b, gains_all, shift, back,
    send, recv, rounds,
):
    local, planes, cols = params_ref.shape
    levels = planes // 2
    members = nm * local
    half = members // 2
    nx = x_size
    nz = nm // nx
    obs = index_ref.shape[1]
    chunk = obs // nx
    cell_planes = planes // nm
    me_mem = lax.axis_index("mem")
    me_space = lax.axis_index("space")
    me_z = me_mem // nx
    me_x = me_mem % nx

    def space_peer(d):
        return {"space": (me_space + d) % ns}

    def x_peer(d):
        peer = (me_x + d) % nx
        return peer, {"mem": me_z * nx + peer}

    def z_peer(d):
        return {"mem": (me_z + d) % nz * nx + me_x}

    barrier = pltpu.get_barrier_semaphore()
    nearby = [space_peer(1), space_peer(ns - 1), z_peer(1), z_peer(nz - 1)]
    greeted = nearby + [x_peer(d)[1] for d in range(1, nx)]
    for device in greeted:
        pl.semaphore_signal(barrier, inc=1, device_id=device)

    for b in range(planes // 8):
        pt[b * 8 : (b + 1) * 8] = jnp.swapaxes(params_ref[:, b * 8 : (b + 1) * 8, :], 0, 1)

    pl.semaphore_wait(barrier, len(greeted))

    def put(src, dst, phase, device):
        pltpu.make_async_remote_copy(
            src_ref=src, dst_ref=dst, send_sem=send.at[phase], recv_sem=recv.at[phase],
            device_id=device,
        ).start()

    def arrived(ref, phase):
        pltpu.make_async_copy(ref, ref, recv.at[phase]).wait()

    def sent(ref, phase):
        pltpu.make_async_copy(ref, ref, send.at[phase]).wait()

    def put_all(pick, dst, phase):
        def body(t, c):
            q = t // nx
            dz = nz // 2 + (1 - 2 * (q % 2)) * ((q + 1) // 2)
            peer = (me_z + dz) % nz * nx + (me_x + t + 1) % nx
            put(pick(peer), dst, phase, {"mem": peer})
            return c

        lax.fori_loop(0, nm - 1, body, 0, unroll=True)

    def greet(devices, step):
        for device in devices:
            pl.semaphore_signal(rounds.at[step], inc=1, device_id=device)

    put(start_ref, up_s, 0, space_peer(1))
    put(start_ref, dn_s, 1, space_peer(ns - 1))
    put(pt.at[pl.ds(levels, levels)], up_p, 2, space_peer(1))
    put(pt.at[pl.ds(0, levels)], dn_p, 3, space_peer(ns - 1))
    greet(nearby, 0)

    def to_chunk(ref, peer):
        return ref.at[:, pl.ds(pl.multiple_of(peer * chunk, chunk), chunk)]

    for d in range(1, nx):
        peer, device = x_peer(d)
        put(to_chunk(noise_ref, peer), noise_x.at[me_x], 4, device)
    noise_x[me_x] = noise_ref[:, pl.ds(pl.multiple_of(me_x * chunk, chunk), chunk)]
    dev[me_mem] = pt[pl.ds(me_mem * cell_planes, cell_planes)]

    pl.semaphore_wait(rounds.at[0], 4)
    greet([space_peer(2), space_peer(ns - 2), z_peer(2), z_peer(nz - 2)], 1)

    def diffusivity(cells):
        return 0.1 + 0.8 / (1.0 + jnp.exp(-cells))

    arrived(up_s, 0)
    arrived(dn_s, 1)
    has_up = me_space > 0
    has_down = me_space < ns - 1
    zero = jnp.zeros((levels, cols), F32)
    state = [
        jnp.where(has_up, up_s[0], zero),
        jnp.where(has_up, up_s[1], zero),
        start_ref[0],
        start_ref[1],
        jnp.where(has_down, dn_s[0], zero),
        jnp.where(has_down, dn_s[1], zero),
    ]
    for r in range(4):
        mid = state[r + 1]
        first_lap[0, r] = mid
        first_lap[1, r] = step_weight * (
            state[r + 2] + state[r] + shifted_cols(mid, 1) + shifted_cols(mid, -1) - 4.0 * mid
        )
    pl.semaphore_wait(rounds.at[1], 4)
    greet([x_peer(d)[1] for d in range(1, nx)], 2)
    arrived(up_p, 2)
    arrived(dn_p, 3)

    for level in range(levels):
        cells = [up_p[level], pt[level], pt[levels + level], dn_p[level]]
        diffs = [diffusivity(c) for c in cells]
        firsts = [
            first_lap[0, r, level : level + 1, :] + diffs[r] * first_lap[1, r, level : level + 1, :]
            for r in range(4)
        ]
        firsts[0] = jnp.where(has_up, firsts[0], 0.0)
        firsts[3] = jnp.where(has_down, firsts[3], 0.0)
        for r in range(2):
            mid = firsts[r + 1]
            lap = firsts[r + 2] + firsts[r] + shifted_cols(mid, 1) + shifted_cols(mid, -1) - 4.0 * mid
            second[r * levels + level] = mid + step_weight * diffs[r + 1] * lap

    blocks = cols // 128
    pieces = []
    for b in range(blocks):
        block = second[:, :, b * 128 : (b + 1) * 128].reshape(planes * local, 128)
        high = block.astype(BF16)
        left = block - high.astype(F32)
        mid = left.astype(BF16)
        low = (left - mid.astype(F32)).astype(BF16)
        pieces.append(jnp.concatenate([high, mid, low], axis=1))
    for c in range(nx):
        where = index_ref[:, c * chunk : (c + 1) * chunk]
        lane_of = where % 128
        block_of = where // 128
        hot = (lax.broadcasted_iota(jnp.int32, (128, chunk), 0) == lane_of).astype(F32).astype(BF16)
        hot = jnp.concatenate([hot, hot, hot], axis=0)
        total = jnp.zeros((local, chunk), F32)
        for b in range(blocks):
            picked = jnp.dot(pieces[b], hot, preferred_element_type=F32)
            for p in range(planes):
                total = total + jnp.where(
                    block_of == p * blocks + b, picked[p * local : (p + 1) * local], 0.0
                )
        predicted_ref[:, c * chunk : (c + 1) * chunk] = total

    pl.semaphore_wait(rounds.at[2], nx - 1)
    put_all(lambda peer: to_chunk(predicted_ref, peer % nx), pred_all.at[me_mem], 5)
    pred_all[me_mem] = predicted_ref[:, pl.ds(pl.multiple_of(me_x * chunk, chunk), chunk)]
    arrived(noise_x.at[pl.ds(0, nx - 1)], 4)
    seen = observed_ref[:, pl.ds(pl.multiple_of(me_x * chunk, chunk), chunk)]
    target = seen + noise_x[...].reshape(nx * local, chunk)
    arrived(pred_all.at[pl.ds(0, nm - 1)], 5)

    everyone = pred_all[...].reshape(members, chunk)
    pred_own = pred_all[pl.ds(me_z * nx, nx)].reshape(nx * local, chunk)
    mean = jnp.sum(everyone, axis=0, keepdims=True) * (1.0 / members)
    spread = everyone - mean
    part_g[...] = product(pred_own - mean, spread, ((1,), (1,))).reshape(nx, local, members)
    for d in range(1, nx):
        peer, device = x_peer(d)
        put(part_g.at[peer], part_gx.at[me_x], 6, device)
    part_m[...] = product(target - pred_own, spread, ((1,), (1,))).reshape(nx, local, members)
    for d in range(1, nx):
        peer, device = x_peer(d)
        put(part_m.at[peer], part_mx.at[me_x], 7, device)
    put_all(lambda peer: pt.at[pl.ds(peer * cell_planes, cell_planes)], dev.at[me_mem], 13)
    part_gx[me_x] = part_g[me_x]
    part_mx[me_x] = part_m[me_x]

    arrived(part_gx.at[pl.ds(0, nx - 1)], 6)
    own_g[...] = jnp.sum(part_gx[...], axis=0)
    for d in range(1, ns):
        put(own_g, part_gs.at[me_space], 8, space_peer(d))
    part_gs[me_space] = own_g[...]
    arrived(part_mx.at[pl.ds(0, nx - 1)], 7)
    own_m[...] = jnp.sum(part_mx[...], axis=0)
    for d in range(1, ns):
        put(own_m, part_ms.at[me_space], 9, space_peer(d))
    part_ms[me_space] = own_m[...]

    arrived(part_gs.at[pl.ds(0, ns - 1)], 8)
    total = jnp.sum(part_gs[...], axis=0) * (1.0 / nobs_all)
    rows_a[...] = total[:, :half]
    rows_b[...] = total[:, half:]
    leading = me_z < nz // 2

    @pl.when(leading)
    def _():
        put_all(lambda peer: rows_a, gram_a.at[me_mem], 10)
        gram_a[me_mem] = rows_a[...]

    put_all(lambda peer: rows_b, gram_b.at[me_mem], 11)
    gram_b[me_mem] = rows_b[...]

    arrived(part_ms.at[pl.ds(0, ns - 1)], 9)
    rows_m[...] = jnp.sum(part_ms[...], axis=0) * (1.0 / nobs_all)
    put_all(lambda peer: rows_m, gains_all.at[me_mem], 12)
    gains_all[me_mem] = rows_m[...]

    @pl.when(leading)
    def _():
        arrived(gram_a.at[pl.ds(0, nm // 2 - 1)], 10)

    @pl.when(jnp.logical_not(leading))
    def _():
        arrived(gram_a, 10)

    eye = lax.broadcasted_iota(jnp.int32, (half, half), 0) == lax.broadcasted_iota(
        jnp.int32, (half, half), 1
    )
    ridge = jnp.where(eye, obs_variance, 0.0)
    inv_a = spd_inverse(gram_a[...].reshape(half, half) + ridge)
    arrived(gram_b.at[pl.ds(0, nm - 1)], 11)
    right = gram_b[...].reshape(members, half)
    upper = right[:half]
    lower = product(upper, inv_a, ((0,), (0,)))
    inv_b = spd_inverse(right[half:] + ridge - mm(lower, upper))

    arrived(dev.at[pl.ds(0, nm - 1)], 13)
    deviation = jnp.concatenate(
        [dev[:, p].reshape(members, cols) for p in range(cell_planes)], axis=1
    )
    deviation = deviation - jnp.sum(deviation, axis=0, keepdims=True) * (1.0 / members)
    dev_a, dev_b = deviation[:half], deviation[half:]
    sol_b = mm(inv_b, dev_b - mm(lower, dev_a))
    sol_a = mm(inv_a, dev_a) - product(lower, sol_b, ((0,), (0,)))
    arrived(gains_all.at[pl.ds(0, nm - 1)], 12)
    gains = gains_all[...].reshape(members, members)
    moved = mm(gains[:, :half], sol_a) + mm(gains[:, half:], sol_b)
    for p in range(cell_planes):
        shift[:, p] = moved[:, p * cols : (p + 1) * cols].reshape(nm, local, cols)

    put_all(lambda peer: shift.at[peer], back.at[pl.ds(me_mem * cell_planes, cell_planes)], 14)
    back[pl.ds(me_mem * cell_planes, cell_planes)] = shift[me_mem]

    sent(start_ref, 0)
    sent(start_ref, 1)
    sent(up_p, 2)
    sent(dn_p, 3)
    sent(noise_x.at[pl.ds(0, nx - 1)], 4)
    sent(pred_all.at[pl.ds(0, nm - 1)], 5)
    sent(part_gx.at[pl.ds(0, nx - 1)], 6)
    sent(part_mx.at[pl.ds(0, nx - 1)], 7)
    sent(part_gs.at[pl.ds(0, ns - 1)], 8)
    sent(part_ms.at[pl.ds(0, ns - 1)], 9)

    @pl.when(leading)
    def _():
        sent(gram_b.at[pl.ds(0, nm - 1)], 10)

    sent(gram_b.at[pl.ds(0, nm - 1)], 11)
    sent(gains_all.at[pl.ds(0, nm - 1)], 12)
    sent(dev.at[pl.ds(0, nm - 1)], 13)
    sent(back.at[pl.ds(0, (nm - 1) * cell_planes)], 14)

    arrived(back.at[pl.ds(0, (nm - 1) * cell_planes)], 14)
    for b in range(planes // 8):
        shift_ref[:, b * 8 : (b + 1) * 8, :] = jnp.swapaxes(back[b * 8 : (b + 1) * 8], 0, 1)


def per_device(params, start_field, obs_index, observed, obs_noise):
    local, rows, levels, cols = params.shape
    nm, ns = lax.axis_size("mem"), lax.axis_size("space")
    obs = obs_index.shape[0]
    members = nm * local
    nx = x_size
    chunk = obs // nx
    planes = rows * levels
    cell_planes = planes // nm
    vmem = pl.BlockSpec(memory_space=pltpu.VMEM)
    half = members // 2
    shapes = [
        (planes, local, cols),
        (nm, cell_planes, local, cols),
        (levels, local, cols),
        (levels, local, cols),
        (rows, levels, cols),
        (rows, levels, cols),
        (2, 4, levels, cols),
        (planes, local, cols),
        (nx, local, chunk),
        (nm, local, chunk),
        (nx, local, members),
        (nx, local, members),
        (nx, local, members),
        (nx, local, members),
        (local, members),
        (local, members),
        (ns, local, members),
        (ns, local, members),
        (local, half),
        (local, half),
        (local, members),
        (nm // 2, local, half),
        (nm, local, half),
        (nm, local, members),
        (nm, cell_planes, local, cols),
        (planes, local, cols),
    ]
    shift, predicted = pl.pallas_call(
        functools.partial(kernel, nm, ns, obs * ns),
        out_shape=(
            jax.ShapeDtypeStruct((local, planes, cols), F32),
            jax.ShapeDtypeStruct((local, obs), F32),
        ),
        in_specs=[vmem] * 5,
        out_specs=(vmem, vmem),
        scratch_shapes=[pltpu.VMEM(s, F32) for s in shapes]
        + [pltpu.SemaphoreType.DMA((15,)), pltpu.SemaphoreType.DMA((15,)), pltpu.SemaphoreType.REGULAR((3,))],
        compiler_params=pltpu.CompilerParams(collective_id=0, has_side_effects=True),
    )(
        params.reshape(local, planes, cols),
        start_field,
        obs_index.reshape(1, obs),
        observed.reshape(1, obs),
        obs_noise,
    )
    return params + shift.reshape(params.shape), predicted


def solution(mesh):
    in_specs = (
        P("mem", "space", None, None),
        P("space", None, None),
        P("space"),
        P("space"),
        P("mem", "space"),
    )
    out_specs = (P("mem", "space", None, None), P("mem", "space"))
    return jax.shard_map(
        per_device, mesh=mesh, in_specs=in_specs, out_specs=out_specs, check_vma=False
    )
```
